32 devices in a mesh: gx: 8 (over z, x), gy: 4 (over y, core).
Axes of the slice: x: 2, y: 2, z: 4, core: 2. Of those that a mesh axis runs over, the one named last changes fastest.
Arguments:
- right_side: float32 [4096, 128], P(('gx', 'gy'))
- compress: float32 [4096, 128], P(('gx', 'gy')), may hold values from 0.5 to 8
- block_fill: int32 [4096], P(('gx', 'gy')), may hold values from 32 to 128, as said below
- pair_home: int32 [12288], P(('gx', 'gy')), may hold values from 0 to 4095, as said below
- pair_far: int32 [12288], P(('gx', 'gy')), may hold values from 0 to 4095, as said below
- pair_count: int32 [32], P(('gx', 'gy')), may hold values from 1 to 384, as said below
- weights: bfloat16 [12288, 128, 128], P(('gx', 'gy')), may hold values from 0 to 0.015625
Outputs:
- solution_field: float32 [4096, 128], P(('gx', 'gy'))
- residual: float32 [4096, 128], P(('gx', 'gy'))
The draws below stay inside these ranges and needn't reach their ends.
Inputs may be any that keep to these rules, and one draw needn't show every extreme that they name: `pair_home`: pair slot s names as first block a block of device s // 384, blocks of device d being d * 128 to d * 128 + 127, devices numbered gx major. `pair_far`: the second block belongs to the slot's device or to one of its eight neighbours on the periodic gx by gy grid of devices. `pair_count`: slots after a device's count are ignored; some devices hold 384. `block_fill`: slots after a block's fill are padding; some block holds 128.
All inputs are finite; a program needn't handle non-finite values.
Results may differ from the reference program's by a relative error of at most 0.015.
Values may be sent and summed in bfloat16 or wider, within the bound.
A program may use at most 64 MiB of HBM per device.

```python
import math
import jax
import jax.numpy as jnp
from jax import lax

TILE = 128
BLK_DEV = 128
PAIRS_DEV = 384
ITERS = 3
NBLK = 4096
NPAIR = 12288
N_GX = 8
N_GY = 4
DEVICES = 32


def draw_right_side(key, part):
    ramp = 1.0 + 2.0 * jnp.arange(NBLK, dtype=jnp.float32)[:, None] / max(NBLK - 1, 1)
    rough = jax.random.normal(key, (NBLK, TILE), jnp.float32)
    return jnp.clip(rough, -4.0, 4.0) * ramp


def draw_block_fill(key, part):
    fill = jax.random.randint(jax.random.fold_in(key, 11), (NBLK,), TILE // 4, TILE + 1)
    where = jax.random.randint(jax.random.fold_in(key, 12), (), 0, NBLK)
    return fill.at[where].set(TILE).astype(jnp.int32)


def draw_pair_home(key, part):
    device = jnp.arange(NPAIR, dtype=jnp.int32) // PAIRS_DEV
    inside = jax.random.randint(jax.random.fold_in(key, 21), (NPAIR,), 0, BLK_DEV)
    return (device * BLK_DEV + inside).astype(jnp.int32)


def draw_pair_far(key, part):
    device = jnp.arange(NPAIR, dtype=jnp.int32) // PAIRS_DEV
    first_index = device // N_GY
    second_index = device % N_GY
    step_first = jax.random.randint(jax.random.fold_in(key, 31), (NPAIR,), -1, 2)
    step_second = jax.random.randint(jax.random.fold_in(key, 32), (NPAIR,), -1, 2)
    target = (first_index + step_first) % N_GX * N_GY + (second_index + step_second) % N_GY
    inside = jax.random.randint(jax.random.fold_in(key, 33), (NPAIR,), 0, BLK_DEV)
    return (target * BLK_DEV + inside).astype(jnp.int32)


def draw_pair_count(key, part):
    device = jnp.arange(DEVICES, dtype=jnp.int32)
    band = jax.random.randint(jax.random.fold_in(key, 41), (), 0, N_GX)
    heavy = (device // N_GY - band) % N_GX < 2
    light = jax.random.randint(jax.random.fold_in(key, 42), (DEVICES,), PAIRS_DEV // 8, PAIRS_DEV // 3 + 1)
    return jnp.where(heavy, PAIRS_DEV, light).astype(jnp.int32)


def steps_of(key, shape, split, smallest, largest):
    def one(position, blocks):
        draws = jax.random.uniform(jax.random.fold_in(jax.random.fold_in(key, 6), position), (blocks,), jnp.float32, smallest / len(split), largest / len(split))
        return jnp.repeat(jnp.exp(draws), shape[position] // blocks).reshape((-1,) + (1,) * (len(shape) - position - 1))

    loudness = one(*split[0])
    for cut in split[1:]:
        loudness = loudness * one(*cut)
    return loudness


def setup_inputs(seed: int = 0) -> dict:
    keys = jax.random.split(jax.random.key(seed), 8)
    return {
        "right_side": draw_right_side(jax.random.fold_in(keys[7], 71), 0),
        "compress": jnp.clip(jnp.exp(math.log(8.0) - 2.7725887 * jax.random.uniform(keys[1], (NBLK, TILE), jnp.float32) ** steps_of(keys[1], (NBLK, TILE), ((0, 32),), -0.2, 0.2)), 0.5, 8.0),
        "block_fill": draw_block_fill(jax.random.fold_in(keys[7], 71), 0),
        "pair_home": draw_pair_home(jax.random.fold_in(keys[7], 71), 0),
        "pair_far": draw_pair_far(jax.random.fold_in(keys[7], 71), 0),
        "pair_count": draw_pair_count(jax.random.fold_in(keys[7], 71), 0),
        "weights": jnp.clip(0.015625 * jax.random.uniform(keys[6], (NPAIR, TILE, TILE), jnp.float32) ** steps_of(keys[6], (NPAIR, TILE, TILE), ((0, 32),), -0.2, 0.2), 0.0, 0.015625).astype(jnp.bfloat16),
    }


def apply_operator(field, compress, live, weights, pair_home, pair_far, slot_live):
    quant = (live * field).astype(jnp.bfloat16).astype(jnp.float32)
    stacks = (weights.reshape(DEVICES, PAIRS_DEV, TILE, TILE), pair_home.reshape(DEVICES, PAIRS_DEV),
              pair_far.reshape(DEVICES, PAIRS_DEV), slot_live.reshape(DEVICES, PAIRS_DEV))

    def one_device(totals, pieces):
        tiles, homes, fars, keep = pieces
        tiles = tiles.astype(jnp.float32)
        row_sum = jnp.sum(tiles, axis=2)
        col_sum = jnp.sum(tiles, axis=1)
        first = quant[homes]
        second = quant[fars]
        toward = jnp.einsum("pij,pj->pi", tiles, second, precision=lax.Precision.HIGHEST)
        backward = jnp.einsum("pij,pi->pj", tiles, first, precision=lax.Precision.HIGHEST)
        term_home = (row_sum * first - toward) * keep[:, None]
        term_far = (col_sum * second - backward) * keep[:, None]
        totals = totals.at[homes].add(term_home).at[fars].add(term_far)
        return totals, None

    pairs_sum, _ = lax.scan(one_device, jnp.zeros((NBLK, TILE), jnp.float32), stacks)
    return compress * field + live * pairs_sum


def reference(right_side, compress, block_fill, pair_home, pair_far, pair_count, weights):
    live = (jnp.arange(TILE, dtype=jnp.int32)[None, :] < block_fill[:, None]).astype(jnp.float32)
    slot_index = jnp.arange(NPAIR, dtype=jnp.int32)
    slot_live = ((slot_index % PAIRS_DEV) < pair_count[slot_index // PAIRS_DEV]).astype(jnp.float32)
    solution_field = jnp.zeros_like(right_side)
    residual = right_side
    direction = right_side
    norm_now = jnp.sum(residual * residual)
    for step in range(ITERS):
        image = apply_operator(direction, compress, live, weights, pair_home, pair_far, slot_live)
        alpha = norm_now / jnp.sum(direction * image)
        solution_field = solution_field + alpha * direction
        residual = residual - alpha * image
        norm_next = jnp.sum(residual * residual)
        direction = residual + (norm_next / norm_now) * direction
        norm_now = norm_next
    return solution_field, residual
```

```python
import functools

import jax
import jax.numpy as jnp
from jax import lax
from jax.experimental import pallas as pl
from jax.experimental.pallas import tpu as pltpu
from jax.sharding import PartitionSpec as P

ITERS = 3
GROUP = 16
MESH = pl.DeviceIdType.MESH
F32 = jnp.float32
BF16 = jnp.bfloat16


def matmul(a, b):
    return jnp.dot(a, b, preferred_element_type=F32)


def halves(value):
    high = value.astype(BF16)
    return high, (value - high.astype(F32)).astype(BF16)


def kernel(
    sizes,
    right_ref,
    compress_ref,
    fill_ref,
    index_ref,
    weights_hbm,
    x_ref,
    r_ref,
    wv,
    onehot_home_t,
    onehot_home,
    onehot_far_t,
    onehot_far,
    mask,
    live,
    degree,
    gathered,
    rows_out,
    rows_sum,
    local,
    w_now,
    nearby,
    give,
    take,
    give_deg,
    take_deg,
    red_y,
    red_x,
    load_sem,
    halo_send,
    halo_recv,
    ret_send,
    ret_recv,
    deg_send,
    deg_recv,
    ry_send,
    ry_recv,
    rx_send,
    rx_recv,
):
    n_x, n_y, chunks = sizes
    blocks, tile = right_ref.shape
    npairs = weights_hbm.shape[0]
    groups = npairs // GROUP
    per_chunk = npairs // chunks
    my_x = lax.axis_index("gx")
    my_y = lax.axis_index("gy")

    loads = [
        pltpu.make_async_copy(
            weights_hbm.at[pl.ds(i * per_chunk, per_chunk)],
            wv.at[pl.ds(i * per_chunk, per_chunk)],
            load_sem.at[i],
        )
        for i in range(chunks)
    ]
    for load in loads:
        load.start()

    def at(dx, dy):
        return (lax.rem(my_x + dx + n_x, n_x), lax.rem(my_y + dy + n_y, n_y))

    friends = {(dx % n_x, dy % n_y) for dx in (-1, 0, 1) for dy in (-1, 0, 1)}
    friends |= {(0, dy) for dy in range(n_y)} | {(dx, 0) for dx in range(n_x)}
    friends = sorted(friends - {(0, 0)})
    barrier = pltpu.get_barrier_semaphore()
    for dx, dy in friends:
        pl.semaphore_signal(barrier, inc=1, device_id=at(dx, dy), device_id_type=MESH)

    around = [n for n in range(9) if n != 4]

    def send(n, src, dst, ssem, rsem):
        return pltpu.make_async_remote_copy(
            src_ref=src,
            dst_ref=dst,
            send_sem=ssem,
            recv_sem=rsem,
            device_id=at(n // 3 - 1, n % 3 - 1),
            device_id_type=MESH,
        )

    def halo(k):
        return [
            send(n, nearby.at[k, 4], nearby.at[k, 8 - n], halo_send.at[k, n], halo_recv.at[k, 8 - n])
            for n in around
        ]

    def returns(k):
        return [
            send(n, give.at[k, n], take.at[k, 8 - n], ret_send.at[k, n], ret_recv.at[k, 8 - n])
            for n in around
        ]

    def degrees():
        return [
            send(n, give_deg.at[n], take_deg.at[8 - n], deg_send.at[n], deg_recv.at[8 - n])
            for n in around
        ]

    fill = jnp.broadcast_to(fill_ref[...].astype(F32), (tile, blocks)).T
    live_now = (lax.broadcasted_iota(jnp.int32, (blocks, tile), 1).astype(F32) < fill).astype(F32)
    live[...] = live_now
    nearby[0, 4] = (live_now * right_ref[...]).astype(BF16)

    pl.semaphore_wait(barrier, len(friends))
    for copy in halo(0):
        copy.start()

    home_row = jnp.broadcast_to(index_ref[0:1, :], (blocks, npairs))
    far_row = jnp.broadcast_to(index_ref[1:2, :], (blocks, npairs))
    which = lax.broadcasted_iota(jnp.int32, (blocks, npairs), 0)
    pick = jnp.where(which == home_row, 1.0, 0.0)
    onehot_home_t[...] = pick.astype(BF16)
    onehot_home[...] = pick.T.astype(BF16)
    for n in range(9):
        pick = jnp.where(which + n * blocks == far_row, 1.0, 0.0)
        onehot_far_t[n * blocks : (n + 1) * blocks, :] = pick.astype(BF16)
        onehot_far[:, n * blocks : (n + 1) * blocks] = pick.T.astype(BF16)
    for p in range(GROUP):
        own = lax.broadcasted_iota(jnp.int32, (GROUP, tile), 0) == p
        mask[:, p * tile : (p + 1) * tile] = jnp.where(own, 1.0, 0.0)

    def group_tiles(g):
        return wv[pl.ds(g * GROUP, GROUP)].reshape(GROUP * tile, tile)

    def rows(g):
        return pl.ds(pl.multiple_of(g * GROUP, GROUP), GROUP)

    def backward_group(first, g, carry):
        x = gathered[rows(g), :]
        spread = mask[...].astype(BF16)
        lhs = jnp.concatenate([x] * GROUP, axis=1) * spread
        if first:
            lhs = jnp.concatenate([lhs, spread], axis=0)
        out = matmul(lhs, group_tiles(g))
        rows_out[rows(g), :] = out[:GROUP]
        if first:
            rows_sum[rows(g), :] = out[GROUP:]
        return carry

    def diagonal(y):
        total = y[:, :tile] * mask[:, :tile]
        for p in range(1, GROUP):
            part = slice(p * tile, (p + 1) * tile)
            total += y[:, part] * mask[:, part]
        return total

    def toward_group(first, g, carry):
        x = gathered[rows(g), :]
        if first:
            x = jnp.concatenate([x, jnp.ones_like(x)], axis=0)
        y = lax.dot_general(
            x, group_tiles(g), (((1,), (1,)), ((), ())), preferred_element_type=F32
        )
        rows_out[rows(g), :] = diagonal(y[:GROUP])
        if first:
            rows_sum[rows(g), :] = diagonal(y[GROUP:])
        return carry

    def scatter(selector, values):
        high, low = halves(values)
        return matmul(selector, high) + matmul(selector, low)

    def operate(k, field, during=None):
        first = k == 0
        gathered[...] = matmul(onehot_home[...], nearby[k, 4]).astype(BF16)
        if first:
            per = groups // chunks
            for i in range(chunks):
                loads[i].wait()
                lax.fori_loop(
                    i * per, (i + 1) * per, functools.partial(backward_group, True), 0, unroll=2
                )
            sums = halves(rows_sum[...])
            for n in range(9):
                select = onehot_far_t[n * blocks : (n + 1) * blocks, :]
                total = matmul(select, sums[0]) + matmul(select, sums[1])
                if n == 4:
                    degree[...] = total
                else:
                    give_deg[n] = total.astype(BF16)
            for copy in degrees():
                copy.start()
        else:
            lax.fori_loop(0, groups, functools.partial(backward_group, False), 0, unroll=2)
        terms = rows_out[...].astype(BF16)
        for n in range(9):
            total = matmul(onehot_far_t[n * blocks : (n + 1) * blocks, :], terms)
            if n == 4:
                local[...] = total
            else:
                give[k, n] = total.astype(BF16)
        for copy in returns(k):
            copy.start()
        if during is not None:
            during()
        for copy in halo(k):
            copy.wait_recv()
        gathered[...] = matmul(onehot_far[...], nearby[k].reshape(9 * blocks, tile)).astype(BF16)
        lax.fori_loop(0, groups, functools.partial(toward_group, first), 0, unroll=2)
        if first:
            degree[...] += scatter(onehot_home_t[...], rows_sum[...])
        total = local[...] + matmul(onehot_home_t[...], rows_out[...].astype(BF16))
        if first:
            for copy in degrees():
                copy.wait_recv()
            for n in around:
                degree[...] += take_deg[n].astype(F32)
        for copy in returns(k):
            copy.wait_recv()
        for n in around:
            total += take[k, n].astype(F32)
        pairs = degree[...] * nearby[k, 4].astype(F32) - total
        return compress_ref[...] * field + live[...] * pairs

    def sum_y(k):
        return [
            pltpu.make_async_remote_copy(
                src_ref=red_y.at[k, my_y],
                dst_ref=red_y.at[k, my_y],
                send_sem=ry_send.at[k, d],
                recv_sem=ry_recv.at[k, n_y - d],
                device_id=at(0, d),
                device_id_type=MESH,
            )
            for d in range(1, n_y)
        ]

    def sum_x(k):
        return [
            pltpu.make_async_remote_copy(
                src_ref=red_x.at[k, my_x],
                dst_ref=red_x.at[k, my_x],
                send_sem=rx_send.at[k, d],
                recv_sem=rx_recv.at[k, n_x - d],
                device_id=at(d, 0),
                device_id_type=MESH,
            )
            for d in range(1, n_x)
        ]

    def sums_start(k, residual, image):
        which_row = lax.broadcasted_iota(jnp.int32, (8, tile), 0)
        norm = jnp.sum(residual * residual, axis=0, keepdims=True)
        along = jnp.sum(residual * image, axis=0, keepdims=True)
        red_y[k, my_y] = jnp.where(which_row == 0, norm, jnp.where(which_row == 1, along, 0.0))
        for copy in sum_y(k):
            copy.start()

    def sums_middle(k):
        for copy in sum_y(k):
            copy.wait_recv()
        red_x[k, my_x] = jnp.sum(red_y[k], axis=0)
        for copy in sum_x(k):
            copy.start()

    def sums_end(k):
        for copy in sum_x(k):
            copy.wait_recv()
        totals = jnp.sum(jnp.sum(red_x[k], axis=0), axis=1, keepdims=True)
        return totals[0:1, :], totals[1:2, :]

    residual = right_ref[...]
    image = operate(0, residual)
    w_now[...] = image
    r_ref[...] = residual
    norm_before = alpha = direction = along = onward = None
    for k in range(ITERS):
        last = k + 1 == ITERS
        sums_start(k, r_ref[...], w_now[...])
        if not last:
            nearby[k + 1, 4] = (live[...] * w_now[...]).astype(BF16)
            for copy in halo(k + 1):
                copy.start()
            further = operate(k + 1, w_now[...], lambda: sums_middle(k))
        else:
            sums_middle(k)
        norm_now, product = sums_end(k)
        residual = r_ref[...]
        image = w_now[...]
        if k == 0:
            alpha = norm_now / product
            direction, along = residual, image
            x_ref[...] = alpha * direction
            if not last:
                onward = further
        else:
            ratio = norm_now / norm_before
            alpha = norm_now / (product - ratio * norm_now / alpha)
            direction = residual + ratio * direction
            along = image + ratio * along
            x_ref[...] += alpha * direction
            if not last:
                onward = further + ratio * onward
        norm_before = norm_now
        r_ref[...] = residual - alpha * along
        if not last:
            w_now[...] = image - alpha * onward

    for k in range(ITERS):
        for copy in halo(k) + returns(k) + sum_y(k) + sum_x(k):
            copy.wait_send()
    for copy in degrees():
        copy.wait_send()


def on_device(mesh_sizes, right_side, compress, block_fill, pair_home, pair_far, pair_count, weights):
    n_x, n_y = mesh_sizes
    blocks, tile = right_side.shape
    npairs = weights.shape[0]
    my_x = lax.axis_index("gx")
    my_y = lax.axis_index("gy")
    keep = jnp.arange(npairs, dtype=jnp.int32) < pair_count[0]
    far_device = pair_far // blocks
    slot_x = (far_device // n_y - my_x + 1) % n_x
    slot_y = (far_device % n_y - my_y + 1) % n_y
    far_slot = (slot_x * 3 + slot_y) * blocks + pair_far % blocks
    home = pair_home - (my_x * n_y + my_y) * blocks
    index = jnp.where(keep, jnp.stack([home, far_slot]), -1)
    chunks = 4
    dma = pltpu.SemaphoreType.DMA
    vmem = pl.BlockSpec(memory_space=pltpu.VMEM)
    out = jax.ShapeDtypeStruct((blocks, tile), F32)
    return pl.pallas_call(
        functools.partial(kernel, (n_x, n_y, chunks)),
        out_shape=(out, out),
        in_specs=[vmem, vmem, vmem, vmem, pl.BlockSpec(memory_space=pl.ANY)],
        out_specs=(vmem, vmem),
        scratch_shapes=[
            pltpu.VMEM((npairs, tile, tile), BF16),
            pltpu.VMEM((blocks, npairs), BF16),
            pltpu.VMEM((npairs, blocks), BF16),
            pltpu.VMEM((9 * blocks, npairs), BF16),
            pltpu.VMEM((npairs, 9 * blocks), BF16),
            pltpu.VMEM((GROUP, GROUP * tile), F32),
            pltpu.VMEM((blocks, tile), F32),
            pltpu.VMEM((blocks, tile), F32),
            pltpu.VMEM((npairs, tile), BF16),
            pltpu.VMEM((npairs, tile), F32),
            pltpu.VMEM((npairs, tile), F32),
            pltpu.VMEM((blocks, tile), F32),
            pltpu.VMEM((blocks, tile), F32),
            pltpu.VMEM((ITERS, 9, blocks, tile), BF16),
            pltpu.VMEM((ITERS, 9, blocks, tile), BF16),
            pltpu.VMEM((ITERS, 9, blocks, tile), BF16),
            pltpu.VMEM((9, blocks, tile), BF16),
            pltpu.VMEM((9, blocks, tile), BF16),
            pltpu.VMEM((ITERS, n_y, 8, tile), F32),
            pltpu.VMEM((ITERS, n_x, 8, tile), F32),
            dma((chunks,)),
            dma((ITERS, 9)),
            dma((ITERS, 9)),
            dma((ITERS, 9)),
            dma((ITERS, 9)),
            dma((9,)),
            dma((9,)),
            dma((ITERS, n_y)),
            dma((ITERS, n_y)),
            dma((ITERS, n_x)),
            dma((ITERS, n_x)),
        ],
        compiler_params=pltpu.CompilerParams(
            collective_id=0, has_side_effects=True, vmem_limit_bytes=56 * 1024 * 1024
        ),
    )(right_side, compress, block_fill[None], index, weights)


def solution(mesh):
    return jax.shard_map(
        functools.partial(on_device, (mesh.shape["gx"], mesh.shape["gy"])),
        mesh=mesh,
        in_specs=(
            P(("gx", "gy"), None),
            P(("gx", "gy"), None),
            P(("gx", "gy")),
            P(("gx", "gy")),
            P(("gx", "gy")),
            P(("gx", "gy")),
            P(("gx", "gy"), None, None),
        ),
        out_specs=(P(("gx", "gy"), None), P(("gx", "gy"), None)),
        check_vma=False,
    )
```

```python
import functools

import jax
import jax.numpy as jnp
from jax import lax
from jax.experimental import pallas as pl
from jax.experimental.pallas import tpu as pltpu
from jax.sharding import PartitionSpec as P

ITERS = 3
GROUP = 16
UNROLL = 3
MESH = pl.DeviceIdType.MESH
F32 = jnp.float32
BF16 = jnp.bfloat16


def matmul(a, b):
    return jnp.dot(a, b, preferred_element_type=F32)


def halves(value):
    high = value.astype(BF16)
    return high, (value - high.astype(F32)).astype(BF16)


def kernel(
    sizes,
    right_ref,
    compress_ref,
    fill_ref,
    home_ref,
    far_ref,
    count_ref,
    weights_hbm,
    x_ref,
    r_ref,
    wv,
    wt,
    onehot_home_t,
    onehot_home,
    onehot_far_t,
    onehot_far,
    mask,
    live,
    degree,
    gathered,
    rows_out,
    rows_sum,
    local,
    w_now,
    nearby,
    give,
    take,
    far_deg,
    give_deg,
    take_deg,
    red_y,
    red_x,
    load_sem,
    halo_send,
    halo_recv,
    ret_send,
    ret_recv,
    deg_send,
    deg_recv,
    ry_send,
    ry_recv,
    rx_send,
    rx_recv,
):
    n_x, n_y, chunks = sizes
    blocks, tile = right_ref.shape
    npairs = weights_hbm.shape[0]
    groups = npairs // GROUP
    per_chunk = npairs // chunks
    my_x = lax.axis_index("gx")
    my_y = lax.axis_index("gy")

    loads = [
        pltpu.make_async_copy(
            weights_hbm.at[pl.ds(i * per_chunk, per_chunk)],
            wv.at[pl.ds(i * per_chunk, per_chunk)],
            load_sem.at[i],
        )
        for i in range(chunks)
    ]
    for load in loads:
        load.start()

    def at(dx, dy):
        return (lax.rem(my_x + dx + n_x, n_x), lax.rem(my_y + dy + n_y, n_y))

    friends = {(dx % n_x, dy % n_y) for dx in (-1, 0, 1) for dy in (-1, 0, 1)}
    friends |= {(0, dy) for dy in range(n_y)} | {(dx, 0) for dx in range(n_x)}
    friends = sorted(friends - {(0, 0)})
    barrier = pltpu.get_barrier_semaphore()
    for dx, dy in friends:
        pl.semaphore_signal(barrier, inc=1, device_id=at(dx, dy), device_id_type=MESH)

    longer = 2 * lax.rem(my_x, 2) - 1
    order = [(longer, dy) for dy in (1, -1, 0)] + [(-longer, dy) for dy in (1, -1, 0)]
    order += [(0, 1), (0, -1)]
    around = [((dx + 1) * 3 + dy + 1, dx, dy) for dx, dy in order]

    def send(to, src, dst, ssem, rsem):
        return pltpu.make_async_remote_copy(
            src_ref=src,
            dst_ref=dst,
            send_sem=ssem,
            recv_sem=rsem,
            device_id=at(to[1], to[2]),
            device_id_type=MESH,
        )

    def halo(k):
        return [
            send(to, nearby.at[k, 4], nearby.at[k, 8 - to[0]], halo_send.at[k, to[0]], halo_recv.at[k, 8 - to[0]])
            for to in around
        ]

    def returns(k):
        return [
            send(to, give.at[k, to[0]], take.at[k, 8 - to[0]], ret_send.at[k, to[0]], ret_recv.at[k, 8 - to[0]])
            for to in around
        ]

    def degrees():
        return [
            send(to, give_deg.at[to[0]], take_deg.at[8 - to[0]], deg_send.at[to[0]], deg_recv.at[8 - to[0]])
            for to in around
        ]

    fill = jnp.broadcast_to(fill_ref[...].astype(F32), (tile, blocks)).T
    live_now = (lax.broadcasted_iota(jnp.int32, (blocks, tile), 1).astype(F32) < fill).astype(F32)
    live[...] = live_now
    nearby[0, 4] = (live_now * right_ref[...]).astype(BF16)

    pl.semaphore_wait(barrier, len(friends))
    for copy in halo(0):
        copy.start()

    keep = lax.broadcasted_iota(jnp.int32, (1, npairs), 1) < count_ref[0]
    home_row = jnp.broadcast_to(jnp.where(keep, home_ref[...], -1), (blocks, npairs))
    far_row = jnp.broadcast_to(jnp.where(keep, far_ref[...], -1), (blocks, npairs))
    which = lax.broadcasted_iota(jnp.int32, (blocks, npairs), 0)
    pick = jnp.where(which + (my_x * n_y + my_y) * blocks == home_row, 1.0, 0.0)
    onehot_home_t[...] = pick.astype(BF16)
    onehot_home[...] = pick.T.astype(BF16)
    for n in range(9):
        far_x, far_y = at(n // 3 - 1, n % 3 - 1)
        pick = jnp.where(which + (far_x * n_y + far_y) * blocks == far_row, 1.0, 0.0)
        onehot_far_t[n * blocks : (n + 1) * blocks, :] = pick.astype(BF16)
        onehot_far[:, n * blocks : (n + 1) * blocks] = pick.T.astype(BF16)
    for p in range(GROUP):
        own = lax.broadcasted_iota(jnp.int32, (GROUP, tile), 0) == p
        mask[:, p * tile : (p + 1) * tile] = jnp.where(own, 1.0, 0.0).astype(BF16)

    def rows(g):
        return pl.ds(pl.multiple_of(g * GROUP, GROUP), GROUP)

    def group_products(first, held, g, carry):
        x = gathered[rows(g), :]
        spread = mask[...]
        lhs = jnp.concatenate([x] * GROUP, axis=1) * spread
        if first:
            lhs = jnp.concatenate([lhs, spread], axis=0)
        out = matmul(lhs, held[pl.ds(g * GROUP, GROUP)].reshape(GROUP * tile, tile))
        rows_out[rows(g), :] = out[:GROUP].astype(BF16)
        if first:
            rows_sum[rows(g), :] = out[GROUP:]
        return carry

    def turned_products(g, carry):
        for p in range(GROUP):
            wt[g * GROUP + p] = wv[g * GROUP + p].T
        return group_products(True, wt, g, carry)

    def operate(k, field, during=None):
        first = k == 0
        gathered[...] = matmul(onehot_home[...], nearby[k, 4]).astype(BF16)
        if first:
            per = groups // chunks
            for i in range(chunks):
                loads[i].wait()
                lax.fori_loop(
                    i * per,
                    (i + 1) * per,
                    functools.partial(group_products, True, wv),
                    0,
                    unroll=UNROLL,
                )
            high, low = halves(rows_sum[...])
            for n in range(9):
                select = onehot_far_t[n * blocks : (n + 1) * blocks, :]
                far_deg[n] = matmul(select, high) + matmul(select, low)
                give_deg[n] = far_deg[n].astype(BF16)
            for copy in halo(k):
                copy.wait_recv()
        else:
            lax.fori_loop(
                0, groups, functools.partial(group_products, False, wv), 0, unroll=UNROLL
            )
        terms = rows_out[...]
        for n in (0, 1, 2, 6, 7, 8, 3, 5, 4):
            total = matmul(onehot_far_t[n * blocks : (n + 1) * blocks, :], terms)
            if first and n != 4:
                total -= far_deg[n] * nearby[k, n].astype(F32)
            if n == 4:
                local[...] = total
            else:
                give[k, n] = total.astype(BF16)
        for copy in returns(k):
            copy.start()
        if first:
            for copy in degrees():
                copy.start()
        if during is not None:
            during()
        if not first:
            for copy in halo(k):
                copy.wait_recv()
        gathered[...] = matmul(onehot_far[...], nearby[k].reshape(9 * blocks, tile)).astype(BF16)
        if first:
            lax.fori_loop(0, groups, turned_products, 0)
            high, low = halves(rows_sum[...])
            select = onehot_home_t[...]
            degree[...] = far_deg[4] + matmul(select, high) + matmul(select, low)
        else:
            lax.fori_loop(
                0, groups, functools.partial(group_products, False, wt), 0, unroll=UNROLL
            )
        total = local[...] + matmul(onehot_home_t[...], rows_out[...])
        if k == 1:
            for copy in degrees():
                copy.wait_recv()
            for n in (0, 1, 2, 3, 5, 6, 7, 8):
                degree[...] += take_deg[n].astype(F32)
        for copy in returns(k):
            copy.wait_recv()
        for n in (0, 1, 2, 3, 5, 6, 7, 8):
            total += take[k, n].astype(F32)
        pairs = degree[...] * nearby[k, 4].astype(F32) - total
        return compress_ref[...] * field + live[...] * pairs

    def sum_y(k):
        return [
            pltpu.make_async_remote_copy(
                src_ref=red_y.at[k, my_y],
                dst_ref=red_y.at[k, my_y],
                send_sem=ry_send.at[k, d],
                recv_sem=ry_recv.at[k, n_y - d],
                device_id=at(0, d),
                device_id_type=MESH,
            )
            for d in range(1, n_y)
        ]

    def sum_x(k):
        return [
            pltpu.make_async_remote_copy(
                src_ref=red_x.at[k, my_x],
                dst_ref=red_x.at[k, my_x],
                send_sem=rx_send.at[k, d],
                recv_sem=rx_recv.at[k, n_x - d],
                device_id=at(d, 0),
                device_id_type=MESH,
            )
            for d in range(1, n_x)
        ]

    def sums_start(k, residual, image):
        which_row = lax.broadcasted_iota(jnp.int32, (8, tile), 0)
        norm = jnp.sum(residual * residual, axis=0, keepdims=True)
        along = jnp.sum(residual * image, axis=0, keepdims=True)
        red_y[k, my_y] = jnp.where(which_row == 0, norm, jnp.where(which_row == 1, along, 0.0))
        for copy in sum_y(k):
            copy.start()

    def sums_middle(k):
        for copy in sum_y(k):
            copy.wait_recv()
        red_x[k, my_x] = jnp.sum(red_y[k], axis=0)
        for copy in sum_x(k):
            copy.start()

    def sums_end(k):
        for copy in sum_x(k):
            copy.wait_recv()
        totals = jnp.sum(jnp.sum(red_x[k], axis=0), axis=1, keepdims=True)
        return totals[0:1, :], totals[1:2, :]

    residual = right_ref[...]
    image = operate(0, residual)
    w_now[...] = image
    r_ref[...] = residual
    norm_before = alpha = direction = along = onward = None
    for k in range(ITERS):
        last = k + 1 == ITERS
        sums_start(k, r_ref[...], w_now[...])
        if not last:
            nearby[k + 1, 4] = (live[...] * w_now[...]).astype(BF16)
            for copy in halo(k + 1):
                copy.start()
            further = operate(k + 1, w_now[...], lambda: sums_middle(k))
        else:
            sums_middle(k)
        norm_now, product = sums_end(k)
        residual = r_ref[...]
        image = w_now[...]
        if k == 0:
            alpha = norm_now / product
            direction, along = residual, image
            x_ref[...] = alpha * direction
            if not last:
                onward = further
        else:
            ratio = norm_now / norm_before
            alpha = norm_now / (product - ratio * norm_now / alpha)
            direction = residual + ratio * direction
            along = image + ratio * along
            x_ref[...] += alpha * direction
            if not last:
                onward = further + ratio * onward
        norm_before = norm_now
        r_ref[...] = residual - alpha * along
        if not last:
            w_now[...] = image - alpha * onward

    for k in range(ITERS):
        for copy in halo(k) + returns(k) + sum_y(k) + sum_x(k):
            copy.wait_send()
    for copy in degrees():
        copy.wait_send()


def on_device(mesh_sizes, right_side, compress, block_fill, pair_home, pair_far, pair_count, weights):
    n_x, n_y = mesh_sizes
    blocks, tile = right_side.shape
    npairs = weights.shape[0]
    chunks = 4
    dma = pltpu.SemaphoreType.DMA
    vmem = pl.BlockSpec(memory_space=pltpu.VMEM)
    out = jax.ShapeDtypeStruct((blocks, tile), F32)
    return pl.pallas_call(
        functools.partial(kernel, (n_x, n_y, chunks)),
        out_shape=(out, out),
        in_specs=[vmem] * 5 + [pl.BlockSpec(memory_space=pltpu.SMEM), pl.BlockSpec(memory_space=pl.ANY)],
        out_specs=(vmem, vmem),
        scratch_shapes=[
            pltpu.VMEM((npairs, tile, tile), BF16),
            pltpu.VMEM((npairs, tile, tile), BF16),
            pltpu.VMEM((blocks, npairs), BF16),
            pltpu.VMEM((npairs, blocks), BF16),
            pltpu.VMEM((9 * blocks, npairs), BF16),
            pltpu.VMEM((npairs, 9 * blocks), BF16),
            pltpu.VMEM((GROUP, GROUP * tile), BF16),
            pltpu.VMEM((blocks, tile), F32),
            pltpu.VMEM((blocks, tile), F32),
            pltpu.VMEM((npairs, tile), BF16),
            pltpu.VMEM((npairs, tile), BF16),
            pltpu.VMEM((npairs, tile), F32),
            pltpu.VMEM((blocks, tile), F32),
            pltpu.VMEM((blocks, tile), F32),
            pltpu.VMEM((ITERS, 9, blocks, tile), BF16),
            pltpu.VMEM((ITERS, 9, blocks, tile), BF16),
            pltpu.VMEM((ITERS, 9, blocks, tile), BF16),
            pltpu.VMEM((9, blocks, tile), F32),
            pltpu.VMEM((9, blocks, tile), BF16),
            pltpu.VMEM((9, blocks, tile), BF16),
            pltpu.VMEM((ITERS, n_y, 8, tile), F32),
            pltpu.VMEM((ITERS, n_x, 8, tile), F32),
            dma((chunks,)),
            dma((ITERS, 9)),
            dma((ITERS, 9)),
            dma((ITERS, 9)),
            dma((ITERS, 9)),
            dma((9,)),
            dma((9,)),
            dma((ITERS, n_y)),
            dma((ITERS, n_y)),
            dma((ITERS, n_x)),
            dma((ITERS, n_x)),
        ],
        compiler_params=pltpu.CompilerParams(
            collective_id=0, has_side_effects=True, vmem_limit_bytes=56 * 1024 * 1024
        ),
    )(right_side, compress, block_fill[None], pair_home[None], pair_far[None], pair_count, weights)


def solution(mesh):
    return jax.shard_map(
        functools.partial(on_device, (mesh.shape["gx"], mesh.shape["gy"])),
        mesh=mesh,
        in_specs=(
            P(("gx", "gy"), None),
            P(("gx", "gy"), None),
            P(("gx", "gy")),
            P(("gx", "gy")),
            P(("gx", "gy")),
            P(("gx", "gy")),
            P(("gx", "gy"), None, None),
        ),
        out_specs=(P(("gx", "gy"), None), P(("gx", "gy"), None)),
        check_vma=False,
    )
```

```python
import functools

import jax
import jax.numpy as jnp
from jax import lax
from jax.experimental import pallas as pl
from jax.experimental.pallas import tpu as pltpu
from jax.sharding import PartitionSpec as P

ITERS = 3
GROUP = 16
UNROLL = 3
MESH = pl.DeviceIdType.MESH
F32 = jnp.float32
BF16 = jnp.bfloat16


def matmul(a, b):
    return jnp.dot(a, b, preferred_element_type=F32)


def halves(value):
    high = value.astype(BF16)
    return high, (value - high.astype(F32)).astype(BF16)


def kernel(
    sizes,
    right_ref,
    compress_ref,
    fill_ref,
    home_ref,
    far_ref,
    count_ref,
    weights_hbm,
    x_ref,
    r_ref,
    wv,
    wt,
    onehot_home_t,
    onehot_home,
    onehot_far_t,
    onehot_far,
    mask,
    live,
    degree,
    gathered,
    rows_out,
    rows_sum,
    local,
    w_now,
    nearby,
    give,
    take,
    far_deg,
    give_deg,
    take_deg,
    red_y,
    red_x,
    load_sem,
    halo_send,
    halo_recv,
    ret_send,
    ret_recv,
    deg_send,
    deg_recv,
    ry_send,
    ry_recv,
    rx_send,
    rx_recv,
):
    n_x, n_y, chunks = sizes
    blocks, tile = right_ref.shape
    npairs = weights_hbm.shape[0]
    groups = npairs // GROUP
    per_chunk = npairs // chunks
    my_x = lax.axis_index("gx")
    my_y = lax.axis_index("gy")

    loads = [
        pltpu.make_async_copy(
            weights_hbm.at[pl.ds(i * per_chunk, per_chunk)],
            wv.at[pl.ds(i * per_chunk, per_chunk)],
            load_sem.at[i],
        )
        for i in range(chunks)
    ]
    for load in loads:
        load.start()

    def at(dx, dy):
        return (lax.rem(my_x + dx + n_x, n_x), lax.rem(my_y + dy + n_y, n_y))

    friends = {(dx % n_x, dy % n_y) for dx in (-1, 0, 1) for dy in (-1, 0, 1)}
    friends |= {(0, dy) for dy in range(n_y)} | {(dx, 0) for dx in range(n_x)}
    friends = sorted(friends - {(0, 0)})
    barrier = pltpu.get_barrier_semaphore()
    for dx, dy in friends:
        pl.semaphore_signal(barrier, inc=1, device_id=at(dx, dy), device_id_type=MESH)

    longer = 2 * lax.rem(my_x, 2) - 1
    order = [(longer, dy) for dy in (1, -1, 0)] + [(-longer, dy) for dy in (1, -1, 0)]
    order += [(0, 1), (0, -1)]
    around = [((dx + 1) * 3 + dy + 1, dx, dy) for dx, dy in order]

    def send(to, src, dst, ssem, rsem):
        return pltpu.make_async_remote_copy(
            src_ref=src,
            dst_ref=dst,
            send_sem=ssem,
            recv_sem=rsem,
            device_id=at(to[1], to[2]),
            device_id_type=MESH,
        )

    def halo(k):
        return [
            send(to, nearby.at[k, 4], nearby.at[k, 8 - to[0]], halo_send.at[k, to[0]], halo_recv.at[k, 8 - to[0]])
            for to in around
        ]

    def returns(k):
        return [
            send(to, give.at[k, to[0]], take.at[k, 8 - to[0]], ret_send.at[k, to[0]], ret_recv.at[k, 8 - to[0]])
            for to in around
        ]

    def degrees():
        return [
            send(to, give_deg.at[to[0]], take_deg.at[8 - to[0]], deg_send.at[to[0]], deg_recv.at[8 - to[0]])
            for to in around
        ]

    fill = jnp.broadcast_to(fill_ref[...].astype(F32), (tile, blocks)).T
    live_now = (lax.broadcasted_iota(jnp.int32, (blocks, tile), 1).astype(F32) < fill).astype(F32)
    live[...] = live_now
    nearby[0, 4] = (live_now * right_ref[...]).astype(BF16)

    keep = lax.broadcasted_iota(jnp.int32, (1, npairs), 1) < count_ref[0]
    home_row = jnp.broadcast_to(jnp.where(keep, home_ref[...], -1), (blocks, npairs))
    far_row = jnp.broadcast_to(jnp.where(keep, far_ref[...], -1), (blocks, npairs))
    which = lax.broadcasted_iota(jnp.int32, (blocks, npairs), 0)
    pick = jnp.where(which + (my_x * n_y + my_y) * blocks == home_row, 1.0, 0.0)
    onehot_home_t[...] = pick.astype(BF16)
    onehot_home[...] = pick.T.astype(BF16)
    for n in range(9):
        far_x, far_y = at(n // 3 - 1, n % 3 - 1)
        pick = jnp.where(which + (far_x * n_y + far_y) * blocks == far_row, 1.0, 0.0)
        onehot_far_t[n * blocks : (n + 1) * blocks, :] = pick.astype(BF16)
        onehot_far[:, n * blocks : (n + 1) * blocks] = pick.T.astype(BF16)
    for p in range(GROUP):
        own = lax.broadcasted_iota(jnp.int32, (GROUP, tile), 0) == p
        mask[:, p * tile : (p + 1) * tile] = jnp.where(own, 1.0, 0.0).astype(BF16)

    pl.semaphore_wait(barrier, len(friends))
    for copy in halo(0):
        copy.start()

    def rows(g):
        return pl.ds(pl.multiple_of(g * GROUP, GROUP), GROUP)

    def group_products(first, held, g, carry):
        x = gathered[rows(g), :]
        spread = mask[...]
        lhs = jnp.concatenate([x] * GROUP, axis=1) * spread
        if first:
            lhs = jnp.concatenate([lhs, spread], axis=0)
        out = matmul(lhs, held[pl.ds(g * GROUP, GROUP)].reshape(GROUP * tile, tile))
        rows_out[rows(g), :] = out[:GROUP].astype(BF16)
        if first:
            rows_sum[rows(g), :] = out[GROUP:]
        return carry

    def turned_products(g, carry):
        for p in range(GROUP):
            wt[g * GROUP + p] = wv[g * GROUP + p].T
        return group_products(True, wt, g, carry)

    def operate(k, field, during=None):
        first = k == 0
        gathered[...] = matmul(onehot_home[...], nearby[k, 4]).astype(BF16)
        if first:
            per = groups // chunks
            for i in range(chunks):
                loads[i].wait()
                lax.fori_loop(
                    i * per,
                    (i + 1) * per,
                    functools.partial(group_products, True, wv),
                    0,
                    unroll=UNROLL,
                )
            high, low = halves(rows_sum[...])
            for n in range(9):
                select = onehot_far_t[n * blocks : (n + 1) * blocks, :]
                far_deg[n] = matmul(select, high) + matmul(select, low)
                give_deg[n] = far_deg[n].astype(BF16)
            for copy in halo(k):
                copy.wait_recv()
        else:
            lax.fori_loop(
                0, groups, functools.partial(group_products, False, wv), 0, unroll=UNROLL
            )
        terms = rows_out[...]
        for n in (0, 1, 2, 6, 7, 8, 3, 5, 4):
            total = matmul(onehot_far_t[n * blocks : (n + 1) * blocks, :], terms)
            if first and n != 4:
                total -= far_deg[n] * nearby[k, n].astype(F32)
            if n == 4:
                local[...] = total
            else:
                give[k, n] = total.astype(BF16)
            if n == 8:
                for copy in returns(k)[:6]:
                    copy.start()
        for copy in returns(k)[6:]:
            copy.start()
        if first:
            for copy in degrees():
                copy.start()
        if during is not None:
            during()
        if not first:
            for copy in halo(k):
                copy.wait_recv()
        gathered[...] = matmul(onehot_far[...], nearby[k].reshape(9 * blocks, tile)).astype(BF16)
        if first:
            lax.fori_loop(0, groups, turned_products, 0)
            high, low = halves(rows_sum[...])
            select = onehot_home_t[...]
            degree[...] = far_deg[4] + matmul(select, high) + matmul(select, low)
        else:
            lax.fori_loop(
                0, groups, functools.partial(group_products, False, wt), 0, unroll=UNROLL
            )
        total = local[...] + matmul(onehot_home_t[...], rows_out[...])
        if k == 1:
            for copy in degrees():
                copy.wait_recv()
            for n in (0, 1, 2, 3, 5, 6, 7, 8):
                degree[...] += take_deg[n].astype(F32)
        for copy in returns(k):
            copy.wait_recv()
        for n in (0, 1, 2, 3, 5, 6, 7, 8):
            total += take[k, n].astype(F32)
        pairs = degree[...] * nearby[k, 4].astype(F32) - total
        return compress_ref[...] * field + live[...] * pairs

    def sum_y(k):
        return [
            pltpu.make_async_remote_copy(
                src_ref=red_y.at[k, my_y],
                dst_ref=red_y.at[k, my_y],
                send_sem=ry_send.at[k, d],
                recv_sem=ry_recv.at[k, n_y - d],
                device_id=at(0, d),
                device_id_type=MESH,
            )
            for d in range(1, n_y)
        ]

    def sum_x(k):
        return [
            pltpu.make_async_remote_copy(
                src_ref=red_x.at[k, my_x],
                dst_ref=red_x.at[k, my_x],
                send_sem=rx_send.at[k, d],
                recv_sem=rx_recv.at[k, n_x - d],
                device_id=at(d, 0),
                device_id_type=MESH,
            )
            for d in range(1, n_x)
        ]

    def sums_start(k, residual, image):
        which_row = lax.broadcasted_iota(jnp.int32, (8, tile), 0)
        norm = jnp.sum(residual * residual, axis=0, keepdims=True)
        along = jnp.sum(residual * image, axis=0, keepdims=True)
        red_y[k, my_y] = jnp.where(which_row == 0, norm, jnp.where(which_row == 1, along, 0.0))
        for copy in sum_y(k):
            copy.start()

    def sums_middle(k):
        for copy in sum_y(k):
            copy.wait_recv()
        red_x[k, my_x] = jnp.sum(red_y[k], axis=0)
        for copy in sum_x(k):
            copy.start()

    def sums_end(k):
        for copy in sum_x(k):
            copy.wait_recv()
        totals = jnp.sum(jnp.sum(red_x[k], axis=0), axis=1, keepdims=True)
        return totals[0:1, :], totals[1:2, :]

    residual = right_ref[...]
    image = operate(0, residual)
    w_now[...] = image
    r_ref[...] = residual
    norm_before = alpha = direction = along = onward = None
    for k in range(ITERS):
        last = k + 1 == ITERS
        if last:
            sums_start(k, r_ref[...], w_now[...])
        else:
            nearby[k + 1, 4] = (live[...] * w_now[...]).astype(BF16)
            for copy in halo(k + 1):
                copy.start()
            sums_start(k, r_ref[...], w_now[...])
            further = operate(k + 1, w_now[...], lambda: sums_middle(k))
        if last:
            sums_middle(k)
        norm_now, product = sums_end(k)
        residual = r_ref[...]
        image = w_now[...]
        if k == 0:
            alpha = norm_now / product
            direction, along = residual, image
            x_ref[...] = alpha * direction
            if not last:
                onward = further
        else:
            ratio = norm_now / norm_before
            alpha = norm_now / (product - ratio * norm_now / alpha)
            direction = residual + ratio * direction
            along = image + ratio * along
            x_ref[...] += alpha * direction
            if not last:
                onward = further + ratio * onward
        norm_before = norm_now
        r_ref[...] = residual - alpha * along
        if not last:
            w_now[...] = image - alpha * onward

    for k in range(ITERS):
        for copy in halo(k) + returns(k) + sum_y(k) + sum_x(k):
            copy.wait_send()
    for copy in degrees():
        copy.wait_send()


def on_device(mesh_sizes, right_side, compress, block_fill, pair_home, pair_far, pair_count, weights):
    n_x, n_y = mesh_sizes
    blocks, tile = right_side.shape
    npairs = weights.shape[0]
    chunks = 4
    dma = pltpu.SemaphoreType.DMA
    vmem = pl.BlockSpec(memory_space=pltpu.VMEM)
    out = jax.ShapeDtypeStruct((blocks, tile), F32)
    return pl.pallas_call(
        functools.partial(kernel, (n_x, n_y, chunks)),
        out_shape=(out, out),
        in_specs=[vmem] * 5 + [pl.BlockSpec(memory_space=pltpu.SMEM), pl.BlockSpec(memory_space=pl.ANY)],
        out_specs=(vmem, vmem),
        scratch_shapes=[
            pltpu.VMEM((npairs, tile, tile), BF16),
            pltpu.VMEM((npairs, tile, tile), BF16),
            pltpu.VMEM((blocks, npairs), BF16),
            pltpu.VMEM((npairs, blocks), BF16),
            pltpu.VMEM((9 * blocks, npairs), BF16),
            pltpu.VMEM((npairs, 9 * blocks), BF16),
            pltpu.VMEM((GROUP, GROUP * tile), BF16),
            pltpu.VMEM((blocks, tile), F32),
            pltpu.VMEM((blocks, tile), F32),
            pltpu.VMEM((npairs, tile), BF16),
            pltpu.VMEM((npairs, tile), BF16),
            pltpu.VMEM((npairs, tile), F32),
            pltpu.VMEM((blocks, tile), F32),
            pltpu.VMEM((blocks, tile), F32),
            pltpu.VMEM((ITERS, 9, blocks, tile), BF16),
            pltpu.VMEM((ITERS, 9, blocks, tile), BF16),
            pltpu.VMEM((ITERS, 9, blocks, tile), BF16),
            pltpu.VMEM((9, blocks, tile), F32),
            pltpu.VMEM((9, blocks, tile), BF16),
            pltpu.VMEM((9, blocks, tile), BF16),
            pltpu.VMEM((ITERS, n_y, 8, tile), F32),
            pltpu.VMEM((ITERS, n_x, 8, tile), F32),
            dma((chunks,)),
            dma((ITERS, 9)),
            dma((ITERS, 9)),
            dma((ITERS, 9)),
            dma((ITERS, 9)),
            dma((9,)),
            dma((9,)),
            dma((ITERS, n_y)),
            dma((ITERS, n_y)),
            dma((ITERS, n_x)),
            dma((ITERS, n_x)),
        ],
        compiler_params=pltpu.CompilerParams(
            collective_id=0, has_side_effects=True, vmem_limit_bytes=56 * 1024 * 1024
        ),
    )(right_side, compress, block_fill[None], pair_home[None], pair_far[None], pair_count, weights)


def solution(mesh):
    return jax.shard_map(
        functools.partial(on_device, (mesh.shape["gx"], mesh.shape["gy"])),
        mesh=mesh,
        in_specs=(
            P(("gx", "gy"), None),
            P(("gx", "gy"), None),
            P(("gx", "gy")),
            P(("gx", "gy")),
            P(("gx", "gy")),
            P(("gx", "gy")),
            P(("gx", "gy"), None, None),
        ),
        out_specs=(P(("gx", "gy"), None), P(("gx", "gy"), None)),
        check_vma=False,
    )
```
